32 devices in a mesh: section: 4 (over z), tensor: 4 (over y, core), dp: 2 (over x).
Axes of the slice: x: 2, y: 2, z: 4, core: 2. Of those that a mesh axis runs over, the one named last changes fastest.
Arguments:
- hidden: bfloat16 [4096, 5120], P(('dp', 'section'), 'tensor'), parts along dimension 0, may hold values from -6 to 6
- queries: bfloat16 [4096, 2560], P(('dp', 'section'), 'tensor'), parts along dimension 0, may hold values from -6 to 6
- key_vectors: bfloat16 [4096, 2560], P(('dp', 'section'), 'tensor'), parts along dimension 0, may hold values from -6 to 6
- value_vectors: bfloat16 [4096, 2560], P(('dp', 'section'), 'tensor'), parts along dimension 0, may hold values from -6 to 6
- gate_logits: float32 [4096, 20], P(('dp', 'section'), 'tensor'), parts along dimension 0, may hold values from -6 to 6
- decay_index: int32 [20], P('tensor'), may hold values from 5 to 15
- norm_gain: float32 [2560], P('tensor'), may hold values from 0.25 to 1.75
- out_weight: bfloat16 [2560, 5120], P('tensor'), may hold values from -0.125 to 0.125
Outputs:
- layer_output: bfloat16 [4096, 5120], P(('dp', 'section'), 'tensor'), parts along dimension 0
The draws below stay inside these ranges and needn't reach their ends.
There are 2 independent parts, one for each index of `dp`. The reference program is written for one: setup_inputs(seed, part) draws one part's arguments, and reference() takes and returns one part's arrays. A program takes and returns all parts, laid end to end along the dimension named above; an argument that names none is the same for every part. Nothing has to cross between parts.
All inputs are finite; a program needn't handle non-finite values.
Results may differ from the reference program's by a relative error of at most 0.0055.
The reference program's roundings to bfloat16 on the way count: a program that leaves them out, or rounds other values in their place, can miss the bound.
Values sent between devices are 32-bit elements; how exact they have to be, the bound alone decides.
No kernel may reach another device: no remote copies, remote signals or barrier semaphores. Data moves between devices by JAX's collectives and lax.ppermute only.
A program may use at most 64 MiB of HBM per device.

```python
import jax
import jax.numpy as jnp
from jax import lax

D = 5120
HD = 128
TOK_DEV = 512
HEADS = 20
TOKENS = 2048
N_SECTION = 4


def plant(result, rng, low, top_value):
    shape = result.shape
    place = [jax.random.randint(jax.random.fold_in(rng, axis), (), 0, shape[axis]) for axis in range(len(shape))]
    result = result.at[tuple(place)].set(low)
    longest = shape.index(max(shape))
    place[longest] = (place[longest] + 1) % shape[longest]
    return result.at[tuple(place)].set(top_value)


def levels(own_key, shape, cuts, low, high):
    factor_of = 1.0
    for dim, blocks in cuts:
        draws = jax.random.uniform(jax.random.fold_in(jax.random.fold_in(own_key, 6), dim), (blocks,), jnp.float32, low / len(cuts), high / len(cuts))
        factor_of = factor_of * jnp.repeat(jnp.exp(draws), shape[dim] // blocks).reshape((-1,) + (1,) * (len(shape) - 1 - dim))
    return factor_of


def scatter_about(key, extent, scale, bound, shards=(), kind=jnp.bfloat16):
    array = jax.random.normal(key, extent, jnp.float32) * scale
    if len(shards) > 0:
        array = levels(key, extent, shards, -0.22, 0.18) * array
    return jnp.clip(array, min=-bound, max=bound).astype(kind)


def setup_inputs(seed: int = 0, part: int = 0) -> dict:
    key_of = jax.random.split(jax.random.key(seed), 9)
    part_splits = jax.random.split(jax.random.fold_in(key_of[8], part), 9)
    return {
        "hidden": scatter_about(part_splits[0], (TOKENS, D), 1.0, 6.0, ((0, 4), (1, 4))),
        "queries": scatter_about(part_splits[1], (TOKENS, HEADS * HD), 1.0, 6.0, ((0, 4), (1, 4))),
        "key_vectors": scatter_about(part_splits[2], (TOKENS, HEADS * HD), 1.0, 6.0, ((0, 4), (1, 4))),
        "value_vectors": scatter_about(part_splits[3], (TOKENS, HEADS * HD), 1.0, 6.0, ((0, 4), (1, 4))),
        "gate_logits": scatter_about(part_splits[4], (TOKENS, HEADS), 1.5, 6.0, ((0, 4), (1, 4)), jnp.float32),
        "decay_index": plant(jax.random.randint(key_of[5], (HEADS,), 5, 16), jax.random.fold_in(key_of[5], 1), 5, 15).astype(jnp.int32),
        "norm_gain": jnp.clip(1.0 + 0.15 * jax.random.normal(key_of[6], (HEADS * HD,), jnp.float32), 0.25, 1.75),
        "out_weight": scatter_about(key_of[7], (HEADS * HD, D), (HEADS * HD) ** -0.5, 0.125, ((0, 4),)),
    }


epsilon = 1e-05

def rotate_heads(vectors, positions):
    half_width = HD // 2
    frequency = 10000.0 ** (-(jnp.arange(half_width, dtype=jnp.float32) * 2.0 / HD))
    angles = positions.astype(jnp.float32)[:, None] * frequency[None, :]
    cosine = jnp.cos(angles)[:, None, :]
    sine_part = jnp.sin(angles)[:, None, :]
    front_half = vectors[..., :half_width]
    back_half = vectors[..., half_width:]
    return jnp.concatenate([front_half * cosine - back_half * sine_part, front_half * sine_part + back_half * cosine], axis=-1)

def block_terms(queries, key_vectors, value_vectors, gate_logits, decay_rate, positions):
    row_count = queries.shape[0]
    heads_count = decay_rate.shape[0]
    log_decay = -decay_rate[None, :] * jax.nn.softplus(gate_logits)
    cumulative = jnp.cumsum(log_decay, axis=0)
    rot_q = rotate_heads(queries.astype(jnp.float32).reshape(row_count, heads_count, HD), positions).astype(jnp.bfloat16)
    rot_k = (rotate_heads(key_vectors.astype(jnp.float32).reshape(row_count, heads_count, HD), positions) * HD ** (-0.5)).astype(jnp.bfloat16)
    value_heads = value_vectors.reshape(row_count, heads_count, HD)
    scores = jnp.einsum('thd,shd->hts', rot_q.astype(jnp.float32), rot_k.astype(jnp.float32))
    column_view = cumulative.T
    decay_gaps = column_view[:, :, None] - column_view[:, None, :]
    causal = jnp.arange(row_count)[:, None] >= jnp.arange(row_count)[None, :]
    weights = jnp.exp(jnp.where(causal[None], decay_gaps, -1e+30))
    masked_scores = (scores * weights).astype(jnp.bfloat16)
    intra_part = jnp.einsum('hts,shd->thd', masked_scores.astype(jnp.float32), value_heads.astype(jnp.float32))
    block_total = cumulative[-1]
    weighted_keys = (rot_k.astype(jnp.float32) * jnp.exp(block_total[None, :] - cumulative)[:, :, None]).astype(jnp.bfloat16)
    block_state = jnp.einsum('shd,she->hde', weighted_keys.astype(jnp.float32), value_heads.astype(jnp.float32))
    return (intra_part, rot_q, cumulative, block_total, block_state)

def finish(intra_part, rot_q, cumulative, incoming, norm_gain):
    row_count, heads_count = cumulative.shape
    rounded_state = lax.optimization_barrier(incoming.astype(jnp.bfloat16))
    carried = jnp.einsum('thd,hde->the', rot_q.astype(jnp.float32), rounded_state.astype(jnp.float32))
    combined = intra_part + jnp.exp(cumulative)[:, :, None] * carried
    average = lax.optimization_barrier(jnp.mean(combined, axis=-1, keepdims=True))
    variance = lax.optimization_barrier(jnp.mean((combined - average) ** 2, axis=-1, keepdims=True))
    normed = (combined - average) * lax.rsqrt(variance + epsilon) * norm_gain.reshape(heads_count, HD)
    return normed.reshape(row_count, heads_count * HD).astype(jnp.bfloat16)

def reference(hidden, queries, key_vectors, value_vectors, gate_logits, decay_index, norm_gain, out_weight):
    decay_rate = 2.0 ** (-decay_index.astype(jnp.float32))
    positions = jnp.arange(TOKENS, dtype=jnp.int32)
    width = HEADS * HD

    def advance(carry_state, pieces):
        block_q, block_k, block_v, block_g, block_p = pieces
        intra_part, rot_q, cumulative, block_total, block_state = block_terms(block_q, block_k, block_v, block_g, decay_rate, block_p)
        retained = finish(intra_part, rot_q, cumulative, carry_state, norm_gain)
        next_state = jnp.exp(block_total)[:, None, None] * carry_state + block_state
        return (next_state, retained)
    start_state = jnp.zeros((HEADS, HD, HD), jnp.float32)
    pieces = (queries.reshape(N_SECTION, TOK_DEV, width), key_vectors.reshape(N_SECTION, TOK_DEV, width), value_vectors.reshape(N_SECTION, TOK_DEV, width), gate_logits.reshape(N_SECTION, TOK_DEV, HEADS), positions.reshape(N_SECTION, TOK_DEV))
    final_state, retained = lax.scan(advance, start_state, pieces)
    retained = retained.reshape(TOKENS, width)
    projected = jnp.dot(retained, out_weight, preferred_element_type=jnp.float32)
    return (hidden.astype(jnp.float32) + projected).astype(jnp.bfloat16)
```

```python
import functools

import numpy as np

import jax
import jax.numpy as jnp
from jax import lax
from jax.experimental import pallas as pl
from jax.experimental.pallas import tpu as pltpu
from jax.sharding import PartitionSpec as P

HD = 128
HALF = HD // 2
EPSILON = 1e-05
LANES = 128
F32 = jnp.float32
BF16 = jnp.bfloat16


VMEM_SPEC = pl.BlockSpec(memory_space=pltpu.VMEM)
SMEM_SPEC = pl.BlockSpec(memory_space=pltpu.SMEM)
ANY_SPEC = pl.BlockSpec(memory_space=pl.ANY)


def angle_tables(row_count, n_section):
    frequency = 10000.0 ** (-(np.arange(HALF, dtype=np.float64) * 2.0 / HD))
    frequency = np.concatenate([frequency, frequency])
    near = np.arange(row_count, dtype=np.float64)[:, None] * frequency[None, :]
    far = (np.arange(n_section, dtype=np.float64) * row_count)[:, None] * frequency[None, :]
    return tuple(f(x).astype(np.float32) for x in (near, far) for f in (np.cos, np.sin))


def rotation(index_ref, near_cos, near_sin, far_cos, far_sin):
    section = index_ref[0]
    cos_far = far_cos[pl.ds(section, 1), :]
    sin_far = far_sin[pl.ds(section, 1), :]
    lane = lax.broadcasted_iota(jnp.int32, (1, HD), 1)
    sign = jnp.where(lane < HALF, -1.0, 1.0)
    cosine = near_cos[...] * cos_far - near_sin[...] * sin_far
    sine = near_cos[...] * (sin_far * sign) + near_sin[...] * (cos_far * sign)
    return cosine, sine


def rotate(x, cosine, sine):
    x = x.astype(F32)
    return x * cosine + pltpu.roll(x, HALF, 1) * sine


def state_kernel(heads, groups, index_ref, decay_ref, gates_ref, k_ref, v_ref, nc, ns, fc, fs, *outs):
    state_refs = outs[: len(groups)]
    row_ref, column_ref, grown_ref, total_ref = outs[len(groups):]
    rows = k_ref.shape[0]
    blocks = rows // LANES
    gates = gates_ref[...]
    if heads < 8:
        gates = jnp.concatenate([gates, jnp.zeros((8 - heads, rows), F32)], axis=0)
    head_row = lax.broadcasted_iota(jnp.int32, (8, LANES), 0)
    exponent = jnp.zeros((8, LANES), F32)
    for h in range(heads):
        exponent = jnp.where(head_row == h, decay_ref[h].astype(F32), exponent)
    rate = jnp.exp2(-exponent)[:, :1]
    soft = jnp.maximum(gates, 0.0) + jnp.log1p(jnp.exp(-jnp.abs(gates)))
    log_decay = -rate * soft
    stacked = jnp.concatenate(
        [log_decay[:, b * LANES : (b + 1) * LANES] for b in range(blocks)], axis=0
    )
    high = stacked.astype(BF16)
    rest = stacked - high.astype(F32)
    middle = rest.astype(BF16)
    low = (rest - middle.astype(F32)).astype(BF16)
    parts = jnp.concatenate([high, middle, low], axis=0)
    upper = (
        lax.broadcasted_iota(jnp.int32, (LANES, LANES), 0)
        <= lax.broadcasted_iota(jnp.int32, (LANES, LANES), 1)
    )
    sums = jnp.dot(
        parts, jnp.where(upper, 1.0, 0.0).astype(BF16), preferred_element_type=F32
    )
    span = 8 * blocks
    sums = sums[:span] + sums[span : 2 * span] + sums[2 * span :]
    offset = jnp.zeros((8, 1), F32)
    pieces = []
    for b in range(blocks):
        piece = sums[8 * b : 8 * b + 8] + offset
        pieces.append(piece)
        offset = piece[:, LANES - 1 :]
    row_ref[...] = jnp.concatenate(pieces, axis=1)
    total_ref[...] = jnp.broadcast_to(jnp.exp(offset), (8, LANES))
    flat = jnp.concatenate(pieces, axis=0)
    ends = jnp.concatenate([offset] * blocks, axis=0)
    pad = jnp.zeros((LANES - span, LANES), F32)
    column = jnp.concatenate([flat, pad], axis=0).T
    grown = jnp.concatenate([jnp.exp(flat), pad], axis=0).T
    fading = jnp.concatenate([jnp.exp(ends - flat), pad], axis=0).T
    for b in range(blocks):
        column_ref[b * LANES : (b + 1) * LANES, :] = column[:, 8 * b : 8 * b + 8]
        grown_ref[b * LANES : (b + 1) * LANES, :] = grown[:, 8 * b : 8 * b + 8]
    cosine, sine = rotation(index_ref, nc, ns, fc, fs)
    cosine = cosine * HD ** (-0.5)
    sine = sine * HD ** (-0.5)
    first = 0
    for state_ref, width in zip(state_refs, groups):
        for i in range(width):
            h = first + i
            cols = slice(h * HD, (h + 1) * HD)
            rot_k = rotate(k_ref[:, cols], cosine, sine).astype(BF16).astype(F32)
            fade = jnp.concatenate(
                [
                    jnp.broadcast_to(fading[:, 8 * b + h : 8 * b + h + 1], (LANES, HD))
                    for b in range(blocks)
                ],
                axis=0,
            )
            weighted = (rot_k * fade).astype(BF16)
            state_ref[i] = lax.dot_general(
                weighted, v_ref[:, cols], (((0,), (0,)), ((), ())), preferred_element_type=F32
            )
        first += width


def intra_kernel(heads, index_ref, q_ref, k_ref, v_ref, row_ref, column_ref, nc, ns, fc, fs, intra_ref, rot_ref):
    rows = q_ref.shape[0]
    block = min(256, rows)
    cosine, sine = rotation(index_ref, nc, ns, fc, fs)
    causal = lax.broadcasted_iota(jnp.int32, (block, block), 0) >= lax.broadcasted_iota(
        jnp.int32, (block, block), 1
    )
    for h in range(heads):
        cols = slice(h * HD, (h + 1) * HD)
        rot_q = rotate(q_ref[:, cols], cosine, sine).astype(BF16)
        rot_k = (rotate(k_ref[:, cols], cosine, sine) * HD ** (-0.5)).astype(BF16)
        rot_ref[:, cols] = rot_q
        for t in range(rows // block):
            own = slice(t * block, (t + 1) * block)
            here = jnp.broadcast_to(column_ref[own, h : h + 1], (block, block))
            total = jnp.zeros((block, HD), F32)
            for s in range(t + 1):
                other = slice(s * block, (s + 1) * block)
                score = lax.dot_general(
                    rot_q[own], rot_k[other], (((1,), (1,)), ((), ())), preferred_element_type=F32
                )
                gap = here - row_ref[h : h + 1, other]
                if s == t:
                    gap = jnp.where(causal, gap, -1e30)
                kept = (score * jnp.exp(gap)).astype(BF16)
                total = total + jnp.dot(kept, v_ref[other, cols], preferred_element_type=F32)
            intra_ref[own, cols] = total


def finish_kernel(
    heads, groups, received, first_rows, index_ref, intra_ref, rot_ref, grown_ref, gain_ref, weight_ref, *rest
):
    state_refs = rest[: received * len(groups)]
    kept_ref, part_ref, weight_vmem, sem = rest[received * len(groups):]
    width = weight_vmem.shape[1]
    copy = pltpu.make_async_copy(
        weight_ref.at[:, pl.ds(pl.multiple_of(index_ref[2] * width, LANES), width)], weight_vmem, sem
    )
    copy.start()
    rows = intra_ref.shape[0]
    chosen = index_ref[1]
    first = 0
    for g, count in enumerate(groups):
        for i in range(count):
            h = first + i
            cols = slice(h * HD, (h + 1) * HD)
            state = jnp.zeros((HD, HD), F32)
            for r in range(received):
                state = jnp.where(chosen == r + 1, state_refs[r * len(groups) + g][i], state)
            carried = jnp.dot(rot_ref[:, cols], state.astype(BF16), preferred_element_type=F32)
            combined = intra_ref[:, cols] + jnp.broadcast_to(
                grown_ref[:, h : h + 1], (rows, HD)
            ) * carried
            average = jnp.mean(combined, axis=-1, keepdims=True)
            centered = combined - average
            variance = jnp.mean(centered * centered, axis=-1, keepdims=True)
            normed = centered * lax.rsqrt(variance + EPSILON) * gain_ref[:, cols]
            kept_ref[:, cols] = normed.astype(BF16)
        first += count
    copy.wait()
    part_ref[...] = jnp.dot(
        kept_ref[:first_rows, :], weight_vmem[...], preferred_element_type=F32
    )


def project_kernel(low, high, index_ref, kept_ref, weight_ref, *rest):
    total = jnp.dot(kept_ref[low:high, :], weight_ref[...], preferred_element_type=F32)
    for extra in rest[:-1]:
        total = total + extra[...].astype(F32)
    rest[-1][...] = total


def project(kept, weight, block, low, high, extras=(), tile=640):
    depth = weight.shape[0]
    width = weight.shape[1] // 4
    tile = min(tile, width)
    steps = width // tile
    rows = high - low
    return pl.pallas_call(
        functools.partial(project_kernel, low, high),
        grid_spec=pltpu.PrefetchScalarGridSpec(
            num_scalar_prefetch=1,
            grid=(steps,),
            in_specs=[
                pl.BlockSpec((kept.shape[0], depth), lambda j, b: (0, 0)),
                pl.BlockSpec((depth, tile), lambda j, b: (0, b[0] * steps + j)),
            ]
            + [pl.BlockSpec((rows, tile), lambda j, b: (0, j)) for _ in extras],
            out_specs=pl.BlockSpec((rows, tile), lambda j, b: (0, j)),
        ),
        out_shape=jax.ShapeDtypeStruct((rows, width), F32),
        cost_estimate=pl.CostEstimate(
            flops=2 * rows * depth * width,
            bytes_accessed=2 * depth * width + 4 * rows * width * (1 + len(extras)),
            transcendentals=0,
        ),
    )(block, kept, weight, *extras)


def pass_states(states, block_total, n_section, section):
    groups = [s.shape[0] for s in states]
    if n_section == 4:
        pairs = ([(0, 1), (1, 0), (2, 3), (3, 2)], [(1, 2), (2, 1)], [(0, 1), (1, 0), (2, 3), (3, 2)])
        received = [[] for _ in pairs]
        first = 0
        for state, width in zip(states, groups):
            decay = block_total[first : first + width, :1][:, :, None]
            sent = state
            for stage, pair in enumerate(pairs):
                if stage:
                    sent = state + decay * received[stage - 1][-1]
                received[stage].append(lax.ppermute(sent, "section", pair))
            first += width
        return received, section
    heads = sum(groups)
    decays = lax.all_gather(block_total[:heads, 0], "section", axis=0)
    own = jnp.concatenate(states, axis=0)
    gathered = lax.all_gather(own, "section", axis=0)

    def advance(carry, piece):
        decay, state = piece
        return decay[:, None, None] * carry + state, carry

    _, entering = lax.scan(advance, jnp.zeros_like(own), (decays, gathered))
    mine = lax.dynamic_index_in_dim(entering, section, 0, keepdims=False)
    parts, first = [], 0
    for width in groups:
        parts.append(mine[first : first + width])
        first += width
    return [parts], jnp.int32(1)


def local(n_section, n_tensor, hidden, queries, key_vectors, value_vectors, gate_logits, decay_index, norm_gain, out_weight):
    rows, width = queries.shape
    heads = decay_index.shape[0]
    columns = hidden.shape[1]
    groups = [heads - heads // 2, heads // 2]
    section = lax.axis_index("section")
    me = lax.axis_index("tensor")
    tables = angle_tables(rows, n_section)
    place = section.astype(jnp.int32).reshape(1)
    decay_index = decay_index.astype(jnp.int32)

    outs = pl.pallas_call(
        functools.partial(state_kernel, heads, groups),
        in_specs=[SMEM_SPEC] * 2 + [VMEM_SPEC] * 7,
        out_specs=[VMEM_SPEC] * (len(groups) + 4),
        out_shape=[jax.ShapeDtypeStruct((g, HD, HD), F32) for g in groups]
        + [
            jax.ShapeDtypeStruct((8, rows), F32),
            jax.ShapeDtypeStruct((rows, 8), F32),
            jax.ShapeDtypeStruct((rows, 8), F32),
            jax.ShapeDtypeStruct((8, LANES), F32),
        ],
    )(place, decay_index, gate_logits.T, key_vectors, value_vectors, *tables)
    states = outs[: len(groups)]
    decay_row, decay_column, grown, block_total = outs[len(groups):]

    received, chosen = pass_states(states, block_total, n_section, section)

    intra, rot_q = pl.pallas_call(
        functools.partial(intra_kernel, heads),
        in_specs=[SMEM_SPEC] + [VMEM_SPEC] * 9,
        out_specs=[VMEM_SPEC] * 2,
        out_shape=[
            jax.ShapeDtypeStruct((rows, width), F32),
            jax.ShapeDtypeStruct((rows, width), BF16),
        ],
        cost_estimate=pl.CostEstimate(
            flops=4 * rows * rows * width, bytes_accessed=12 * rows * width, transcendentals=rows * rows * heads
        ),
    )(place, queries, key_vectors, value_vectors, decay_row, decay_column, *tables)

    flat = [piece for stage in received for piece in stage]
    first_rows = rows // 4
    cross = (me ^ 3) if n_tensor == 4 else jnp.int32(0)
    where = jnp.stack([section, chosen, cross]).astype(jnp.int32)
    kept, part = pl.pallas_call(
        functools.partial(finish_kernel, heads, groups, len(received), first_rows),
        in_specs=[SMEM_SPEC] + [VMEM_SPEC] * 4 + [ANY_SPEC] + [VMEM_SPEC] * len(flat),
        out_specs=[VMEM_SPEC] * 2,
        out_shape=[
            jax.ShapeDtypeStruct((rows, width), BF16),
            jax.ShapeDtypeStruct((first_rows, columns), F32),
        ],
        scratch_shapes=[pltpu.VMEM((width, columns), BF16), pltpu.SemaphoreType.DMA],
    )(where, intra, rot_q, grown, norm_gain[None, :], out_weight, *flat)

    if n_tensor != 4:
        product = lax.dot_general(kept, out_weight, (((1,), (0,)), ((), ())), preferred_element_type=F32)
        summed = lax.psum_scatter(product, "tensor", scatter_dimension=1, tiled=True)
        return (hidden.astype(F32) + summed).astype(BF16)

    def swap(x, bit):
        return lax.ppermute(x, "tensor", [(i, i ^ bit) for i in range(n_tensor)])

    def block_of(bit):
        return (me ^ bit).astype(jnp.int32).reshape(1)

    cuts = [0, first_rows, rows * 5 // 8, rows * 7 // 8, rows]
    crossing = [swap(part, 1)]
    others = project(kept, out_weight, block_of(3), first_rows, rows)
    crossing_rest = swap(others, 1)
    arrived = []
    for i, (low, high) in enumerate(zip(cuts[:-1], cuts[1:])):
        extra = crossing[0] if i == 0 else crossing_rest[low - first_rows : high - first_rows]
        arrived.append(swap(project(kept, out_weight, block_of(2), low, high, (extra,)), 2))
    near = swap(project(kept, out_weight, block_of(1), 0, rows), 1)
    own = project(kept, out_weight, block_of(0), 0, rows, (hidden, near))
    return jnp.concatenate(
        [
            (own[low:high] + far).astype(BF16)
            for low, high, far in zip(cuts[:-1], cuts[1:], arrived)
        ],
        axis=0,
    )


def solution(mesh):
    rows = P(("dp", "section"), "tensor")
    placed = (rows, rows, rows, rows, rows, P("tensor"), P("tensor"), P("tensor", None))
    body = functools.partial(local, mesh.shape["section"], mesh.shape["tensor"])
    return jax.shard_map(body, mesh=mesh, in_specs=placed, out_specs=rows, check_vma=False)
```

```python
import functools

import numpy as np

import jax
import jax.numpy as jnp
from jax import lax
from jax.experimental import pallas as pl
from jax.experimental.pallas import tpu as pltpu
from jax.sharding import PartitionSpec as P


HD = 128
HALF = HD // 2
EPSILON = 1e-05
LANES = 128
F32 = jnp.float32
BF16 = jnp.bfloat16


VMEM_SPEC = pl.BlockSpec(memory_space=pltpu.VMEM)
SMEM_SPEC = pl.BlockSpec(memory_space=pltpu.SMEM)
ANY_SPEC = pl.BlockSpec(memory_space=pl.ANY)


def angle_tables(row_count, n_section):
    frequency = 10000.0 ** (-(np.arange(HALF, dtype=np.float64) * 2.0 / HD))
    frequency = np.concatenate([frequency, frequency])
    near = np.arange(row_count, dtype=np.float64)[:, None] * frequency[None, :]
    far = (np.arange(n_section, dtype=np.float64) * row_count)[:, None] * frequency[None, :]
    return tuple(f(x).astype(np.float32) for x in (near, far) for f in (np.cos, np.sin))


def rotation(index_ref, near_cos, near_sin, far_cos, far_sin):
    section = index_ref[0]
    cos_far = far_cos[pl.ds(section, 1), :]
    sin_far = far_sin[pl.ds(section, 1), :]
    lane = lax.broadcasted_iota(jnp.int32, (1, HD), 1)
    sign = jnp.where(lane < HALF, -1.0, 1.0)
    cosine = near_cos[...] * cos_far - near_sin[...] * sin_far
    sine = near_cos[...] * (sin_far * sign) + near_sin[...] * (cos_far * sign)
    return cosine, sine


def rotate(x, cosine, sine):
    x = x.astype(F32)
    return x * cosine + pltpu.roll(x, HALF, 1) * sine


def state_kernel(heads, groups, index_ref, decay_ref, gates_ref, k_ref, v_ref, nc, ns, fc, fs, *outs):
    state_refs = outs[: len(groups)]
    total_refs = outs[len(groups) : 2 * len(groups)]
    row_ref, column_ref, grown_ref = outs[2 * len(groups) :]
    rows = k_ref.shape[0]
    blocks = rows // LANES
    gates = gates_ref[...]
    if heads < 8:
        gates = jnp.concatenate([gates, jnp.zeros((8 - heads, rows), F32)], axis=0)
    head_row = lax.broadcasted_iota(jnp.int32, (8, LANES), 0)
    exponent = jnp.zeros((8, LANES), F32)
    for h in range(heads):
        exponent = jnp.where(head_row == h, decay_ref[h].astype(F32), exponent)
    rate = jnp.exp2(-exponent)[:, :1]
    soft = jnp.maximum(gates, 0.0) + jnp.log1p(jnp.exp(-jnp.abs(gates)))
    log_decay = -rate * soft
    stacked = jnp.concatenate(
        [log_decay[:, b * LANES : (b + 1) * LANES] for b in range(blocks)], axis=0
    )
    high = stacked.astype(BF16)
    rest = stacked - high.astype(F32)
    middle = rest.astype(BF16)
    low = (rest - middle.astype(F32)).astype(BF16)
    parts = jnp.concatenate([high, middle, low], axis=0)
    upper = (
        lax.broadcasted_iota(jnp.int32, (LANES, LANES), 0)
        <= lax.broadcasted_iota(jnp.int32, (LANES, LANES), 1)
    )
    sums = jnp.dot(
        parts, jnp.where(upper, 1.0, 0.0).astype(BF16), preferred_element_type=F32
    )
    span = 8 * blocks
    sums = sums[:span] + sums[span : 2 * span] + sums[2 * span :]
    offset = jnp.zeros((8, 1), F32)
    pieces = []
    for b in range(blocks):
        piece = sums[8 * b : 8 * b + 8] + offset
        pieces.append(piece)
        offset = piece[:, LANES - 1 :]
    row_ref[...] = jnp.concatenate(pieces, axis=1)
    totals = jnp.broadcast_to(jnp.exp(offset), (8, LANES))
    flat = jnp.concatenate(pieces, axis=0)
    ends = jnp.concatenate([offset] * blocks, axis=0)
    pad = jnp.zeros((LANES - span, LANES), F32)
    column = jnp.concatenate([flat, pad], axis=0).T
    grown = jnp.concatenate([jnp.exp(flat), pad], axis=0).T
    fading = jnp.concatenate([jnp.exp(ends - flat), pad], axis=0).T
    for b in range(blocks):
        column_ref[b * LANES : (b + 1) * LANES, :] = column[:, 8 * b : 8 * b + 8]
        grown_ref[b * LANES : (b + 1) * LANES, :] = grown[:, 8 * b : 8 * b + 8]
    cosine, sine = rotation(index_ref, nc, ns, fc, fs)
    cosine = cosine * HD ** (-0.5)
    sine = sine * HD ** (-0.5)
    first = 0
    for state_ref, total_ref, width in zip(state_refs, total_refs, groups):
        for i in range(width):
            h = first + i
            total_ref[i] = totals[h : h + 1]
            cols = slice(h * HD, (h + 1) * HD)
            rot_k = rotate(k_ref[:, cols], cosine, sine).astype(BF16).astype(F32)
            fade = jnp.concatenate(
                [
                    jnp.broadcast_to(fading[:, 8 * b + h : 8 * b + h + 1], (LANES, HD))
                    for b in range(blocks)
                ],
                axis=0,
            )
            weighted = (rot_k * fade).astype(BF16)
            state_ref[i] = lax.dot_general(
                weighted, v_ref[:, cols], (((0,), (0,)), ((), ())), preferred_element_type=F32
            )
        first += width


def intra_kernel(heads, index_ref, q_ref, k_ref, v_ref, row_ref, column_ref, nc, ns, fc, fs, intra_ref, rot_ref):
    rows = q_ref.shape[0]
    block = min(256, rows)
    cosine, sine = rotation(index_ref, nc, ns, fc, fs)
    causal = lax.broadcasted_iota(jnp.int32, (block, block), 0) >= lax.broadcasted_iota(
        jnp.int32, (block, block), 1
    )
    for h in range(heads):
        cols = slice(h * HD, (h + 1) * HD)
        rot_q = rotate(q_ref[:, cols], cosine, sine).astype(BF16)
        rot_k = (rotate(k_ref[:, cols], cosine, sine) * HD ** (-0.5)).astype(BF16)
        rot_ref[:, cols] = rot_q
        for t in range(rows // block):
            own = slice(t * block, (t + 1) * block)
            here = jnp.broadcast_to(column_ref[own, h : h + 1], (block, block))
            total = jnp.zeros((block, HD), F32)
            for s in range(t + 1):
                other = slice(s * block, (s + 1) * block)
                score = lax.dot_general(
                    rot_q[own], rot_k[other], (((1,), (1,)), ((), ())), preferred_element_type=F32
                )
                gap = here - row_ref[h : h + 1, other]
                if s == t:
                    gap = jnp.where(causal, gap, -1e30)
                kept = (score * jnp.exp(gap)).astype(BF16)
                total = total + jnp.dot(kept, v_ref[other, cols], preferred_element_type=F32)
            intra_ref[own, cols] = total


def finish_kernel(heads, groups, received, low, high, index_ref, block_ref, intra_ref, rot_ref, grown_ref, gain_ref, weight_ref, *rest):
    states = received * len(groups)
    state_refs = rest[:states]
    earlier_refs = rest[states:-4]
    kept_ref, part_ref, weight_vmem, sem = rest[-4:]
    width = weight_vmem.shape[1]
    copy = pltpu.make_async_copy(
        weight_ref.at[:, pl.ds(pl.multiple_of(block_ref[0] * width, LANES), width)], weight_vmem, sem
    )
    copy.start()
    chosen = index_ref[0]
    first = 0
    for g, count in enumerate(groups):
        for i in range(count):
            h = first + i
            cols = slice(h * HD, (h + 1) * HD)
            state = jnp.zeros((HD, HD), F32)
            for r in range(received):
                state = jnp.where(chosen == r + 1, state_refs[r * len(groups) + g][i], state)
            carried = jnp.dot(rot_ref[low:high, cols], state.astype(BF16), preferred_element_type=F32)
            combined = intra_ref[low:high, cols] + jnp.broadcast_to(
                grown_ref[low:high, h : h + 1], (high - low, HD)
            ) * carried
            average = jnp.mean(combined, axis=-1, keepdims=True)
            centered = combined - average
            variance = jnp.mean(centered * centered, axis=-1, keepdims=True)
            gain = gain_ref[cols].reshape(1, HD)
            normed = centered * lax.rsqrt(variance + EPSILON) * gain
            kept_ref[kept_ref.shape[0] - (high - low) :, cols] = normed.astype(BF16)
        first += count
    if earlier_refs:
        kept_ref[:low, :] = earlier_refs[0][...]
    copy.wait()
    part_ref[...] = jnp.dot(
        kept_ref[kept_ref.shape[0] - (high - low) :, :], weight_vmem[...], preferred_element_type=F32
    )


def finish(groups, chosen, block, intra, rot_q, grown, gain, weight, received, earlier, low, high, columns):
    width = rot_q.shape[1]
    flat = [piece for stage in received for piece in stage]
    earlier = [] if earlier is None else [earlier]
    size = high if earlier else high - low
    return pl.pallas_call(
        functools.partial(finish_kernel, sum(groups), groups, len(received), low, high),
        in_specs=[SMEM_SPEC] * 2 + [VMEM_SPEC] * 4 + [ANY_SPEC] + [VMEM_SPEC] * len(flat + earlier),
        out_specs=[VMEM_SPEC] * 2,
        out_shape=[
            jax.ShapeDtypeStruct((size, width), BF16),
            jax.ShapeDtypeStruct((high - low, columns), F32),
        ],
        scratch_shapes=[pltpu.VMEM((width, columns), BF16), pltpu.SemaphoreType.DMA],
        cost_estimate=pl.CostEstimate(
            flops=2 * (high - low) * width * columns,
            bytes_accessed=2 * width * columns + 4 * (high - low) * (columns + 2 * width),
            transcendentals=0,
        ),
    )(chosen, block, intra, rot_q, grown, gain, weight, *flat, *earlier)


def project_kernel(cuts, extras, block_ref, kept_ref, weight_ref, *rest):
    low, high = cuts[0], cuts[-1]
    total = jnp.dot(kept_ref[low:high, :], weight_ref[...], preferred_element_type=F32)
    for extra in rest[:extras]:
        total = total + extra[...].astype(F32)
    for out_ref, a, b in zip(rest[extras:], cuts[:-1], cuts[1:]):
        out_ref[...] = total[a - low : b - low]


def project(kept, weight, block, cuts, columns, extras=(), tile=640):
    depth = weight.shape[0]
    tile = min(tile, columns)
    steps = columns // tile
    rows = cuts[-1] - cuts[0]
    spans = [b - a for a, b in zip(cuts[:-1], cuts[1:])]
    return pl.pallas_call(
        functools.partial(project_kernel, cuts, len(extras)),
        grid_spec=pltpu.PrefetchScalarGridSpec(
            num_scalar_prefetch=1,
            grid=(steps,),
            in_specs=[
                pl.BlockSpec((cuts[-1], depth), lambda j, b: (0, 0)),
                pl.BlockSpec((depth, tile), lambda j, b: (0, b[0] * steps + j)),
            ]
            + [pl.BlockSpec((rows, tile), lambda j, b: (0, j)) for _ in extras],
            out_specs=[pl.BlockSpec((n, tile), lambda j, b: (0, j)) for n in spans],
        ),
        out_shape=[jax.ShapeDtypeStruct((n, columns), F32) for n in spans],
        cost_estimate=pl.CostEstimate(
            flops=2 * rows * depth * columns,
            bytes_accessed=2 * depth * columns + 4 * rows * columns * (1 + len(extras)),
            transcendentals=0,
        ),
    )(block, kept, weight, *extras)


def pass_states(states, totals, n_section, n_dp, section):
    if n_section == 4:
        outer, inner = {0: 1, 1: 0, 2: 3, 3: 2}, {1: 2, 2: 1}
        received = [[] for _ in range(3)]
        for state, decay in zip(states, totals):
            sent = state
            for stage, partner in enumerate((outer, inner, outer)):
                if stage:
                    sent = state + decay * received[stage - 1][-1]
                pairs = [
                    (z * n_dp + d, partner[z] * n_dp + d if z in partner else z * n_dp + (d ^ 1) % n_dp)
                    for z in range(n_section)
                    for d in range(n_dp)
                ]
                received[stage].append(lax.ppermute(sent, ("section", "dp"), pairs))
        return received, section
    own = jnp.concatenate(states, axis=0)
    decays = lax.all_gather(jnp.concatenate(totals, axis=0)[:, 0, 0], "section", axis=0)
    gathered = lax.all_gather(own, "section", axis=0)

    def advance(carry, piece):
        decay, state = piece
        return decay[:, None, None] * carry + state, carry

    _, entering = lax.scan(advance, jnp.zeros_like(own), (decays, gathered))
    mine = lax.dynamic_index_in_dim(entering, section, 0, keepdims=False)
    parts, first = [], 0
    for state in states:
        parts.append(mine[first : first + state.shape[0]])
        first += state.shape[0]
    return [parts], jnp.int32(1)


def local(n_section, n_tensor, n_dp, hidden, queries, key_vectors, value_vectors, gate_logits, decay_index, norm_gain, out_weight):
    rows, width = queries.shape
    heads = decay_index.shape[0]
    columns = hidden.shape[1]
    groups = [heads - heads // 2, heads // 2]
    section = lax.axis_index("section").astype(jnp.int32)
    me = lax.axis_index("tensor").astype(jnp.int32)
    tables = angle_tables(rows, n_section)
    place = section.reshape(1)

    outs = pl.pallas_call(
        functools.partial(state_kernel, heads, groups),
        in_specs=[SMEM_SPEC] * 2 + [VMEM_SPEC] * 7,
        out_specs=[VMEM_SPEC] * (2 * len(groups) + 3),
        out_shape=[jax.ShapeDtypeStruct((g, HD, HD), F32) for g in groups]
        + [jax.ShapeDtypeStruct((g, 1, LANES), F32) for g in groups]
        + [
            jax.ShapeDtypeStruct((8, rows), F32),
            jax.ShapeDtypeStruct((rows, 8), F32),
            jax.ShapeDtypeStruct((rows, 8), F32),
        ],
    )(place, decay_index.astype(jnp.int32), gate_logits.T, key_vectors, value_vectors, *tables)
    states = outs[: len(groups)]
    totals = outs[len(groups) : 2 * len(groups)]
    decay_row, decay_column, grown = outs[2 * len(groups) :]

    received, chosen = pass_states(states, totals, n_section, n_dp, section)

    intra, rot_q = pl.pallas_call(
        functools.partial(intra_kernel, heads),
        in_specs=[SMEM_SPEC] + [VMEM_SPEC] * 9,
        out_specs=[VMEM_SPEC] * 2,
        out_shape=[
            jax.ShapeDtypeStruct((rows, width), F32),
            jax.ShapeDtypeStruct((rows, width), BF16),
        ],
        cost_estimate=pl.CostEstimate(
            flops=4 * rows * rows * width, bytes_accessed=12 * rows * width, transcendentals=rows * rows * heads
        ),
    )(place, queries, key_vectors, value_vectors, decay_row, decay_column, *tables)

    def block_of(bit):
        return (me ^ bit).reshape(1) if n_tensor == 4 else jnp.zeros((1,), jnp.int32)

    start = rows * 3 // 8
    common = (groups, chosen.reshape(1), block_of(3), intra, rot_q, grown, norm_gain, out_weight, received)
    kept, part = finish(*common, None, 0, start, columns)

    if n_tensor != 4:
        kept, _ = finish(*common, kept, start, rows, columns)
        product = lax.dot_general(kept, out_weight, (((1,), (0,)), ((), ())), preferred_element_type=F32)
        summed = lax.psum_scatter(product, "tensor", scatter_dimension=1, tiled=True)
        return (hidden.astype(F32) + summed).astype(BF16)

    def swap(x, bit):
        return lax.ppermute(x, "tensor", [(i, i ^ bit) for i in range(n_tensor)])

    cuts = [start, rows * 5 // 8, rows * 7 // 8, rows]
    part = swap(part, 1)
    (lead,) = project(kept, out_weight, block_of(2), [0, start], columns)
    lead = lead + part
    arrived = [swap(lead, 2)]
    kept, rest = finish(*common, kept, start, rows, columns)
    rest = swap(rest, 1)
    (near,) = project(kept, out_weight, block_of(1), [0, rows], columns)
    near = swap(near, 1)
    crossing = project(kept, out_weight, block_of(2), cuts, columns, (rest,))
    for piece in crossing:
        arrived.append(swap(piece, 2))
    (own,) = project(kept, out_weight, block_of(0), [0, rows], columns, (hidden, near))
    result = None
    for low, far in zip([0] + cuts, arrived):
        high = low + far.shape[0]
        piece = (own[low:high] + far).astype(BF16)
        if result is None:
            result = jnp.pad(piece, ((0, rows - high), (0, 0)))
        else:
            result = lax.dynamic_update_slice(result, piece, (low, 0))
    return result


def solution(mesh):
    rows = P(("dp", "section"), "tensor")
    placed = (rows, rows, rows, rows, rows, P("tensor"), P("tensor"), P("tensor", None))

    def body(*arrays):
        return local(*(mesh.shape[n] for n in ("section", "tensor", "dp")), *arrays)

    return jax.shard_map(body, mesh=mesh, in_specs=placed, out_specs=rows, check_vma=False)
```

```python
import functools

import numpy as np

import jax
import jax.numpy as jnp
from jax import lax
from jax.experimental import pallas as pl
from jax.experimental.pallas import tpu as pltpu
from jax.sharding import PartitionSpec as P


HD = 128
HALF = HD // 2
EPSILON = 1e-05
LANES = 128
F32 = jnp.float32
BF16 = jnp.bfloat16


VMEM_SPEC = pl.BlockSpec(memory_space=pltpu.VMEM)
SMEM_SPEC = pl.BlockSpec(memory_space=pltpu.SMEM)
ANY_SPEC = pl.BlockSpec(memory_space=pl.ANY)


def angle_tables(row_count, n_section):
    frequency = 10000.0 ** (-(np.arange(HALF, dtype=np.float64) * 2.0 / HD))
    frequency = np.concatenate([frequency, frequency])
    near = np.arange(row_count, dtype=np.float64)[:, None] * frequency[None, :]
    far = (np.arange(n_section, dtype=np.float64) * row_count)[:, None] * frequency[None, :]
    return tuple(f(x).astype(np.float32) for x in (near, far) for f in (np.cos, np.sin))


def rotation(index_ref, near_cos, near_sin, far_cos, far_sin):
    section = index_ref[0]
    cos_far = far_cos[pl.ds(section, 1), :]
    sin_far = far_sin[pl.ds(section, 1), :]
    lane = lax.broadcasted_iota(jnp.int32, (1, HD), 1)
    sign = jnp.where(lane < HALF, -1.0, 1.0)
    cosine = near_cos[...] * cos_far - near_sin[...] * sin_far
    sine = near_cos[...] * (sin_far * sign) + near_sin[...] * (cos_far * sign)
    return cosine, sine


def rotate(x, cosine, sine):
    x = x.astype(F32)
    return x * cosine + pltpu.roll(x, HALF, 1) * sine


def state_kernel(heads, groups, index_ref, decay_ref, gates_ref, k_ref, v_ref, nc, ns, fc, fs, *outs):
    state_refs = outs[: len(groups)]
    total_refs = outs[len(groups) : 2 * len(groups)]
    row_ref, column_ref, grown_ref = outs[2 * len(groups) :]
    rows = k_ref.shape[0]
    blocks = rows // LANES
    gates = gates_ref[...]
    if heads < 8:
        gates = jnp.concatenate([gates, jnp.zeros((8 - heads, rows), F32)], axis=0)
    head_row = lax.broadcasted_iota(jnp.int32, (8, LANES), 0)
    exponent = jnp.zeros((8, LANES), F32)
    for h in range(heads):
        exponent = jnp.where(head_row == h, decay_ref[h].astype(F32), exponent)
    rate = jnp.exp2(-exponent)[:, :1]
    soft = jnp.maximum(gates, 0.0) + jnp.log1p(jnp.exp(-jnp.abs(gates)))
    log_decay = -rate * soft
    stacked = jnp.concatenate(
        [log_decay[:, b * LANES : (b + 1) * LANES] for b in range(blocks)], axis=0
    )
    high = stacked.astype(BF16)
    rest = stacked - high.astype(F32)
    middle = rest.astype(BF16)
    low = (rest - middle.astype(F32)).astype(BF16)
    parts = jnp.concatenate([high, middle, low], axis=0)
    upper = (
        lax.broadcasted_iota(jnp.int32, (LANES, LANES), 0)
        <= lax.broadcasted_iota(jnp.int32, (LANES, LANES), 1)
    )
    sums = jnp.dot(
        parts, jnp.where(upper, 1.0, 0.0).astype(BF16), preferred_element_type=F32
    )
    span = 8 * blocks
    sums = sums[:span] + sums[span : 2 * span] + sums[2 * span :]
    offset = jnp.zeros((8, 1), F32)
    pieces = []
    for b in range(blocks):
        piece = sums[8 * b : 8 * b + 8] + offset
        pieces.append(piece)
        offset = piece[:, LANES - 1 :]
    row_ref[...] = jnp.concatenate(pieces, axis=1)
    totals = jnp.broadcast_to(jnp.exp(offset), (8, LANES))
    flat = jnp.concatenate(pieces, axis=0)
    ends = jnp.concatenate([offset] * blocks, axis=0)
    pad = jnp.zeros((LANES - span, LANES), F32)
    column = jnp.concatenate([flat, pad], axis=0).T
    grown = jnp.concatenate([jnp.exp(flat), pad], axis=0).T
    fading = jnp.concatenate([jnp.exp(ends - flat), pad], axis=0).T
    for b in range(blocks):
        column_ref[b * LANES : (b + 1) * LANES, :] = column[:, 8 * b : 8 * b + 8]
        grown_ref[b * LANES : (b + 1) * LANES, :] = grown[:, 8 * b : 8 * b + 8]
    cosine, sine = rotation(index_ref, nc, ns, fc, fs)
    cosine = cosine * HD ** (-0.5)
    sine = sine * HD ** (-0.5)
    first = 0
    for state_ref, total_ref, width in zip(state_refs, total_refs, groups):
        for i in range(width):
            h = first + i
            total_ref[i] = totals[h : h + 1]
            cols = slice(h * HD, (h + 1) * HD)
            rot_k = rotate(k_ref[:, cols], cosine, sine).astype(BF16).astype(F32)
            fade = jnp.concatenate(
                [
                    jnp.broadcast_to(fading[:, 8 * b + h : 8 * b + h + 1], (LANES, HD))
                    for b in range(blocks)
                ],
                axis=0,
            )
            weighted = (rot_k * fade).astype(BF16)
            state_ref[i] = lax.dot_general(
                weighted, v_ref[:, cols], (((0,), (0,)), ((), ())), preferred_element_type=F32
            )
        first += width


def intra_kernel(heads, index_ref, q_ref, k_ref, v_ref, row_ref, column_ref, nc, ns, fc, fs, intra_ref, rot_ref):
    rows = q_ref.shape[0]
    block = min(256, rows)
    cosine, sine = rotation(index_ref, nc, ns, fc, fs)
    causal = lax.broadcasted_iota(jnp.int32, (block, block), 0) >= lax.broadcasted_iota(
        jnp.int32, (block, block), 1
    )
    for h in range(heads):
        cols = slice(h * HD, (h + 1) * HD)
        rot_q = rotate(q_ref[:, cols], cosine, sine).astype(BF16)
        rot_k = (rotate(k_ref[:, cols], cosine, sine) * HD ** (-0.5)).astype(BF16)
        rot_ref[:, cols] = rot_q
        for t in range(rows // block):
            own = slice(t * block, (t + 1) * block)
            here = jnp.broadcast_to(column_ref[own, h : h + 1], (block, block))
            total = jnp.zeros((block, HD), F32)
            for s in range(t + 1):
                other = slice(s * block, (s + 1) * block)
                score = lax.dot_general(
                    rot_q[own], rot_k[other], (((1,), (1,)), ((), ())), preferred_element_type=F32
                )
                gap = here - row_ref[h : h + 1, other]
                if s == t:
                    gap = jnp.where(causal, gap, -1e30)
                kept = (score * jnp.exp(gap)).astype(BF16)
                total = total + jnp.dot(kept, v_ref[other, cols], preferred_element_type=F32)
            intra_ref[own, cols] = total


def spread_kernel(row_ref, block_ref, other_ref, same_in, other_in, *outs):
    half = outs[0].shape[0]
    for i, source in enumerate((same_in, other_in)):
        for j in range(2):
            outs[2 * i + j][...] = source[j * half : (j + 1) * half, :].astype(F32)


def spread(weight, quarter, same, other, columns):
    rows = weight.shape[0] // 4
    return pl.pallas_call(
        spread_kernel,
        grid_spec=pltpu.PrefetchScalarGridSpec(
            num_scalar_prefetch=3,
            grid=(1,),
            in_specs=[
                pl.BlockSpec((rows, columns), lambda i, q, s, o: (q[0], s[0])),
                pl.BlockSpec((rows, columns), lambda i, q, s, o: (q[0], o[0])),
            ],
            out_specs=[pl.BlockSpec((rows // 2, columns), lambda i, q, s, o: (0, 0))] * 4,
        ),
        out_shape=[jax.ShapeDtypeStruct((rows // 2, columns), F32)] * 4,
    )(quarter, same, other, weight, weight)


def widen_kernel(block_ref, weight_ref, out_ref):
    out_ref[...] = weight_ref[...].astype(F32)


def widen(weight, block, columns, tile=128):
    depth = weight.shape[0]
    return pl.pallas_call(
        widen_kernel,
        grid_spec=pltpu.PrefetchScalarGridSpec(
            num_scalar_prefetch=1,
            grid=(depth // tile,),
            in_specs=[pl.BlockSpec((tile, columns), lambda i, b: (i, b[0]))],
            out_specs=pl.BlockSpec((tile, columns), lambda i, b: (i, 0)),
        ),
        out_shape=jax.ShapeDtypeStruct((depth, columns), F32),
    )(block, weight)


def finish_kernel(heads, groups, received, index_ref, intra_ref, rot_ref, grown_ref, gain_ref, *rest):
    state_refs, (kept_ref, *wide_refs) = rest[: received * len(groups)], rest[received * len(groups) :]
    rows = intra_ref.shape[0]
    size = rows // len(wide_refs)
    chosen = index_ref[0]
    first = 0
    for g, count in enumerate(groups):
        for i in range(count):
            h = first + i
            cols = slice(h * HD, (h + 1) * HD)
            state = jnp.zeros((HD, HD), F32)
            for r in range(received):
                state = jnp.where(chosen == r + 1, state_refs[r * len(groups) + g][i], state)
            carried = jnp.dot(rot_ref[:, cols], state.astype(BF16), preferred_element_type=F32)
            combined = intra_ref[:, cols] + jnp.broadcast_to(
                grown_ref[:, h : h + 1], (rows, HD)
            ) * carried
            average = jnp.mean(combined, axis=-1, keepdims=True)
            centered = combined - average
            variance = jnp.mean(centered * centered, axis=-1, keepdims=True)
            gain = gain_ref[cols].reshape(1, HD)
            normed = (centered * lax.rsqrt(variance + EPSILON) * gain).astype(BF16)
            kept_ref[:, cols] = normed
            for p, wide_ref in enumerate(wide_refs):
                wide_ref[:, cols] = normed[p * size : (p + 1) * size].astype(F32)
        first += count


def finish(groups, chosen, intra, rot_q, grown, gain, received, parts):
    rows, width = rot_q.shape
    flat = [piece for stage in received for piece in stage]
    return pl.pallas_call(
        functools.partial(finish_kernel, sum(groups), groups, len(received)),
        in_specs=[SMEM_SPEC] + [VMEM_SPEC] * (4 + len(flat)),
        out_specs=[VMEM_SPEC] * (1 + parts),
        out_shape=[jax.ShapeDtypeStruct((rows, width), BF16)]
        + [jax.ShapeDtypeStruct((rows // parts, width), F32)] * parts,
    )(chosen, intra, rot_q, grown, gain, *flat)


def chip_kernel(parts, block_ref, kept_ref, weight_ref, wide_ref, hidden_ref, *rest):
    total = jnp.dot(kept_ref[...], weight_ref[...], preferred_element_type=F32)
    total = total + hidden_ref[...].astype(F32)
    wide = wide_ref[...].astype(BF16)
    size = kept_ref.shape[0] // parts
    for p in range(parts):
        rest[parts + p][...] = total[p * size : (p + 1) * size] + jnp.dot(
            rest[p][...].astype(BF16), wide, preferred_element_type=F32
        )


def chip_sum(kept, weight, block, wide, hidden, pieces, tile=640):
    depth = weight.shape[0]
    rows, columns = hidden.shape
    parts = len(pieces)
    steps = columns // tile
    return pl.pallas_call(
        functools.partial(chip_kernel, parts),
        grid_spec=pltpu.PrefetchScalarGridSpec(
            num_scalar_prefetch=1,
            grid=(steps,),
            in_specs=[
                pl.BlockSpec((rows, depth), lambda j, b: (0, 0)),
                pl.BlockSpec((depth, tile), lambda j, b: (0, b[0] * steps + j)),
                pl.BlockSpec((depth, tile), lambda j, b: (0, j)),
                pl.BlockSpec((rows, tile), lambda j, b: (0, j)),
            ]
            + [pl.BlockSpec((rows // parts, depth), lambda j, b: (0, 0))] * parts,
            out_specs=[pl.BlockSpec((rows // parts, tile), lambda j, b: (0, j))] * parts,
        ),
        out_shape=[jax.ShapeDtypeStruct((rows // parts, columns), F32)] * parts,
    )(block, kept, weight, wide, hidden, *pieces)


def gather_kernel(bits, n_rows, n_sources, quarter_ref, *refs):
    totals = refs[:n_rows]
    sources = refs[n_rows : n_rows + n_rows * n_sources]
    pieces = refs[n_rows * (1 + n_sources) : n_rows * (1 + n_sources) + 2 * n_sources * len(bits)]
    outs = refs[len(refs) - 1 - (len(refs) - 1 - n_rows * (1 + n_sources) - len(pieces)) : -1]
    padded = refs[-1]
    half = pieces[0].shape[0]
    sums = [total[...] for total in totals]
    slot = 0
    for b, bit in enumerate(bits):
        quarter = quarter_ref[0] ^ bit
        start = pl.multiple_of(quarter * LANES, LANES)
        skip = pl.multiple_of(quarter * (2 * half - LANES), 32)
        for n in range(n_sources):
            padded[slot] = jnp.zeros(padded.shape[1:], BF16)
            for j in range(2):
                padded[slot, pl.ds(skip + j * half, half), :] = pieces[
                    2 * (b * n_sources + n) + j
                ][...].astype(BF16)
            for i in range(n_rows):
                window = sources[i * n_sources + n][:, pl.ds(start, 2 * LANES)].astype(BF16)
                sums[i] = sums[i] + jnp.dot(window, padded[slot], preferred_element_type=F32)
            slot += 1
    if len(outs) == n_rows:
        for out, value in zip(outs, sums):
            out[...] = value.astype(out.dtype)
    else:
        size = sums[0].shape[0]
        for i, value in enumerate(sums):
            outs[0][i * size : (i + 1) * size, :] = value.astype(outs[0].dtype)


def gather_sum(totals, sources, pieces, bits, quarter, joined, tile=640):
    rows, columns = totals[0].shape
    width = sources[0][0].shape[1]
    n_rows, n_sources = len(sources), len(sources[0])
    half = pieces[0][0][0].shape[0]
    flat = [x for b in pieces for n in b for x in n]
    if joined:
        out_shape = [jax.ShapeDtypeStruct((n_rows * rows, columns), BF16)]
    else:
        out_shape = [jax.ShapeDtypeStruct((rows, columns), F32)] * n_rows
    return pl.pallas_call(
        functools.partial(gather_kernel, bits, n_rows, n_sources),
        grid_spec=pltpu.PrefetchScalarGridSpec(
            num_scalar_prefetch=1,
            grid=(columns // tile,),
            in_specs=[pl.BlockSpec((rows, tile), lambda j, q: (0, j))] * n_rows
            + [pl.BlockSpec((rows, width), lambda j, q: (0, 0))] * (n_rows * n_sources)
            + [pl.BlockSpec((half, tile), lambda j, q: (0, j))] * len(flat),
            out_specs=[pl.BlockSpec((x.shape[0], tile), lambda j, q: (0, j)) for x in out_shape],
            scratch_shapes=[pltpu.VMEM((n_sources * len(bits), 2 * LANES, tile), BF16)],
        ),
        out_shape=out_shape,
    )(quarter, *totals, *[x for row in sources for x in row], *flat)


def pass_states(states, totals, n_section, n_dp, section):
    if n_section == 4:
        outer, inner = {0: 1, 1: 0, 2: 3, 3: 2}, {1: 2, 2: 1}
        received = [[] for _ in range(3)]
        for state, decay in zip(states, totals):
            sent = state
            for stage, partner in enumerate((outer, inner, outer)):
                if stage:
                    sent = state + decay * received[stage - 1][-1]
                pairs = [
                    (z * n_dp + d, partner[z] * n_dp + d if z in partner else z * n_dp + (d ^ 1) % n_dp)
                    for z in range(n_section)
                    for d in range(n_dp)
                ]
                received[stage].append(lax.ppermute(sent, ("section", "dp"), pairs))
        return received, section
    own = jnp.concatenate(states, axis=0)
    decays = lax.all_gather(jnp.concatenate(totals, axis=0)[:, 0, 0], "section", axis=0)
    gathered = lax.all_gather(own, "section", axis=0)

    def advance(carry, piece):
        decay, state = piece
        return decay[:, None, None] * carry + state, carry

    _, entering = lax.scan(advance, jnp.zeros_like(own), (decays, gathered))
    mine = lax.dynamic_index_in_dim(entering, section, 0, keepdims=False)
    parts, first = [], 0
    for state in states:
        parts.append(mine[first : first + state.shape[0]])
        first += state.shape[0]
    return [parts], jnp.int32(1)


def local(n_section, n_tensor, n_dp, hidden, queries, key_vectors, value_vectors, gate_logits, decay_index, norm_gain, out_weight):
    rows, width = queries.shape
    heads = decay_index.shape[0]
    columns = hidden.shape[1]
    groups = [heads - heads // 2, heads // 2]
    section = lax.axis_index("section").astype(jnp.int32)
    me = lax.axis_index("tensor").astype(jnp.int32)
    tables = angle_tables(rows, n_section)
    place = section.reshape(1)

    gathers = n_tensor == 4 and n_dp == 2 and n_section % 2 == 0 and width == 5 * LANES
    sizes = {"tensor": n_tensor, "section": n_section, "dp": n_dp}

    def swap(x, axis, bit):
        return lax.ppermute(x, axis, [(i, i ^ bit) for i in range(sizes[axis])])

    def block_of(bit):
        return (me ^ bit).reshape(1)

    if gathers:
        quarter = (2 * lax.axis_index("dp").astype(jnp.int32) + section % 2).reshape(1)
        sent = spread(out_weight, quarter, block_of(2), block_of(3), columns)
        pieces = {"y": [[swap(sent[2 * n + j], "tensor", 2 + n) for j in range(2)] for n in range(2)]}
        pieces["x"] = [[swap(pieces["y"][n][j], "dp", 1) for j in range(2)] for n in range(2)]
        pieces["z"] = [[swap(pieces["y"][n][j], "section", 1) for j in range(2)] for n in range(2)]
        pieces["d"] = [
            [swap(pieces["z"][0][j], "dp", 1) for j in range(2)],
            [swap(pieces["x"][1][j], "section", 1) for j in range(2)],
        ]

    outs = pl.pallas_call(
        functools.partial(state_kernel, heads, groups),
        in_specs=[SMEM_SPEC] * 2 + [VMEM_SPEC] * 7,
        out_specs=[VMEM_SPEC] * (2 * len(groups) + 3),
        out_shape=[jax.ShapeDtypeStruct((g, HD, HD), F32) for g in groups]
        + [jax.ShapeDtypeStruct((g, 1, LANES), F32) for g in groups]
        + [
            jax.ShapeDtypeStruct((8, rows), F32),
            jax.ShapeDtypeStruct((rows, 8), F32),
            jax.ShapeDtypeStruct((rows, 8), F32),
        ],
    )(place, decay_index.astype(jnp.int32), gate_logits.T, key_vectors, value_vectors, *tables)
    states = outs[: len(groups)]
    totals = outs[len(groups) : 2 * len(groups)]
    decay_row, decay_column, grown = outs[2 * len(groups) :]

    received, chosen = pass_states(states, totals, n_section, n_dp, section)

    intra, rot_q = pl.pallas_call(
        functools.partial(intra_kernel, heads),
        in_specs=[SMEM_SPEC] + [VMEM_SPEC] * 9,
        out_specs=[VMEM_SPEC] * 2,
        out_shape=[
            jax.ShapeDtypeStruct((rows, width), F32),
            jax.ShapeDtypeStruct((rows, width), BF16),
        ],
        cost_estimate=pl.CostEstimate(
            flops=4 * rows * rows * width, bytes_accessed=12 * rows * width, transcendentals=rows * rows * heads
        ),
    )(place, queries, key_vectors, value_vectors, decay_row, decay_column, *tables)

    parts = 2
    kept, *wide = finish(groups, chosen.reshape(1), intra, rot_q, grown, norm_gain, received, parts)
    if not gathers:
        product = lax.dot_general(kept, out_weight, (((1,), (0,)), ((), ())), preferred_element_type=F32)
        summed = lax.psum_scatter(product, "tensor", scatter_dimension=1, tiled=True)
        return (hidden.astype(F32) + summed).astype(BF16)

    beside = widen(out_weight, block_of(1), columns)
    beside = swap(beside, "tensor", 1)
    far_wide = [swap(x, "tensor", 2) for x in wide]
    chip_wide = [swap(x, "tensor", 1) for x in wide]
    totals = chip_sum(kept, out_weight, block_of(0), beside, hidden, chip_wide)
    across = [swap(x, "tensor", 1) for x in far_wide]
    sources = [[x, y] for x, y in zip(far_wide, across)]
    early, late = [pieces[k] for k in "yxz"], [pieces["d"]]
    totals = list(totals)
    for i in range(parts):
        totals[i : i + 1] = gather_sum(totals[i : i + 1], sources[i : i + 1], early, (0, 2, 1), quarter, False)
    (result,) = gather_sum(totals, sources, late, (3,), quarter, True)
    return result


def solution(mesh):
    rows = P(("dp", "section"), "tensor")
    placed = (rows, rows, rows, rows, rows, P("tensor"), P("tensor"), P("tensor", None))

    def body(*arrays):
        return local(*(mesh.shape[n] for n in ("section", "tensor", "dp")), *arrays)

    return jax.shard_map(body, mesh=mesh, in_specs=placed, out_specs=rows, check_vma=False)
```
